128 devices in a mesh: chan: 16 (over y_lo, x, core), day: 8 (over y_hi, z).
Axes of the slice: x: 4, y: 4 (y_hi: 2, y_lo: 2; y = y_hi * 2 + y_lo), z: 4, core: 2. Of those that a mesh axis runs over, the one named last changes fastest.
Arguments:
- spectra: bfloat16 [8, 4, 48, 3, 2, 4096], P('day', None, None, None, None, 'chan'), may hold values from -6 to 6
- clean_counts: int32 [8], replicated, may hold values from 1 to 48, as said below
- window_mask: int32 [8, 48, 32], P('day', None, 'chan'), may hold values 0 or 1
Outputs:
- stacks: bfloat16 [8, 4, 2, 4096, 2304], P('day', None, None, 'chan')
The draws below stay inside these ranges and needn't reach their ends.
Inputs may be any that keep to these rules, and one draw needn't show every extreme that they name: `clean_counts`: some day has exactly 48 clean windows.
All inputs are finite; a program needn't handle non-finite values. No bound on the sum of `window_mask` on one device may be relied on, other than what follows from the above.
Results may differ from the reference program's by a relative error of at most 0.001.
Values may be sent and summed in bfloat16 or wider, within the bound.
No kernel may reach another device: no remote copies, remote signals or barrier semaphores. Data moves between devices by JAX's collectives and lax.ppermute only.
A program may use at most 128 MiB of HBM per device.

```python
import jax
import jax.numpy as jnp
from jax import lax

CHAN_DEV = 256
CHANNELS = 4096
GROUP = 128
GROUPS = 32
DAYS = 8
BINS = 4
WIN = 48
SEG = 3
SPAN = 5
LAGS = 2304
N_CHAN = 16


def draw_clean_counts(key, part):
    first_key = jax.random.fold_in(key, 11)
    second_key = jax.random.fold_in(key, 23)
    base_counts = jax.random.randint(first_key, (DAYS,), max(1, WIN // 12), WIN // 2)
    busy_day = jax.random.randint(second_key, (), 0, DAYS)
    return jnp.where(jnp.arange(DAYS) == busy_day, WIN, base_counts).astype(jnp.int32)


def with_ends(array, stream_key, least, largest):
    dims = array.shape
    place = [jax.random.randint(jax.random.fold_in(stream_key, axis), (), 0, dims[axis]) for axis in range(len(dims))]
    array = array.at[tuple(place)].set(least)
    longest = dims.index(max(dims))
    place[longest] = (place[longest] + 1) % dims[longest]
    return array.at[tuple(place)].set(largest)


def shard_levels(rng, extent, shards, smallest, largest):
    gain, own = 1.0, jax.random.fold_in(rng, 6)
    for axis_at, shards_of in shards:
        steps = jnp.exp(jax.random.uniform(jax.random.fold_in(own, axis_at), (shards_of,), jnp.float32, smallest / len(shards), largest / len(shards)))
        gain = gain * jnp.repeat(steps, extent[axis_at] // shards_of).reshape([-1 if axis == axis_at else 1 for axis in range(len(extent))])
    return gain


def centred(stream_key, dims, spread, reach, split=(), held_as=jnp.bfloat16):
    factor_of = shard_levels(stream_key, dims, split, -0.22, 0.18) if split else 1.0
    entries = jax.random.normal(stream_key, dims, jnp.float32) * spread * factor_of
    return jnp.minimum(jnp.maximum(entries, -reach), reach).astype(held_as)


def setup_inputs(seed: int = 0) -> dict:
    splits = jax.random.split(jax.random.key(seed), 4)
    spectra = centred(splits[0], (DAYS, BINS, WIN, SEG, 2, CHANNELS), 1.0, 6.0, ((0, 8), (5, 16)))
    clean_counts = draw_clean_counts(jax.random.fold_in(splits[3], 71), 0)
    window_mask = with_ends((jax.random.randint(splits[2], (DAYS, WIN, GROUPS), 0, 4) < 3).astype(jnp.int32), jax.random.fold_in(splits[2], 1), 0, 1)
    return {"spectra": spectra, "clean_counts": clean_counts, "window_mask": window_mask}


def reference(spectra, clean_counts, window_mask):
    in_count = (jnp.arange(WIN, dtype=jnp.int32)[None, :] < clean_counts[:, None]).astype(jnp.int32)
    keeper = window_mask * in_count[:, :, None]
    keep_chan = jnp.repeat(keeper, GROUP, axis=2)
    masked = spectra * keep_chan[:, None, :, None, None, :].astype(jnp.bfloat16)
    flipped = jnp.stack([masked[:, :, :, :, 1, :], -masked[:, :, :, :, 0, :]], axis=4)
    row_view = masked.reshape(DAYS, BINS, WIN * SEG * 2, CHANNELS)
    flip_view = flipped.reshape(DAYS, BINS, WIN * SEG * 2, CHANNELS)
    wrapped = jnp.concatenate([row_view, row_view[..., :LAGS]], axis=-1)
    half_span = SPAN // 2
    all_days = []
    for d in range(DAYS):
        def one_group(group_index):
            first_col = (group_index * CHAN_DEV).astype(jnp.int32)
            summed = jnp.zeros((BINS, 2 * CHAN_DEV, LAGS), jnp.float32)
            for offset in range(-half_span, half_span + 1):
                e = d + offset
                if e < 0 or e >= DAYS:
                    continue
                left_real = lax.dynamic_slice_in_dim(row_view[e], first_col, CHAN_DEV, 2)
                left_imag = lax.dynamic_slice_in_dim(flip_view[e], first_col, CHAN_DEV, 2)
                left_part = jnp.concatenate([left_real, left_imag], axis=-1).astype(jnp.float32)
                right_part = lax.dynamic_slice_in_dim(wrapped[e], first_col, LAGS, 2).astype(jnp.float32)
                product = jnp.einsum("bki,bkj->bij", left_part, right_part)
                weight_day = jnp.float32(1.0) / (SEG * clean_counts[e].astype(jnp.float32))
                summed = summed + weight_day * product
            return summed.astype(jnp.bfloat16)

        group_tiles = lax.map(one_group, jnp.arange(N_CHAN, dtype=jnp.int32))
        group_tiles = group_tiles.reshape(N_CHAN, BINS, 2, CHAN_DEV, LAGS)
        group_tiles = jnp.transpose(group_tiles, (1, 2, 0, 3, 4)).reshape(BINS, 2, CHANNELS, LAGS)
        all_days.append(group_tiles)
    return jnp.stack(all_days, axis=0)
```

```python
import functools

import jax
import jax.numpy as jnp
from jax import lax
from jax.experimental import pallas as pl
from jax.experimental.pallas import tpu as pltpu
from jax.sharding import PartitionSpec as P

GROUP = 128
BINS = 4
WIN = 48
SEG = 3
SPAN = 5
ROWS = WIN * SEG * 2
OWN = 128
CLASSES = (512, 640, 768, 1408)
BIN_CHUNKS = ((0, 2), (2, 2))


AXES = ("chan", "day")
bf16 = jnp.bfloat16
f32 = jnp.float32


def pairs(chan_to, day_to):
    route = []
    for c in range(16):
        for d in range(8):
            c2 = chan_to(c // 8, (c // 2) % 4, c % 2)
            d2 = day_to(d)
            if 0 <= d2 < 8:
                route.append((c * 8 + d, ((c2[0] * 4 + c2[1]) * 2 + c2[2]) * 8 + d2))
    return route


def keep(y, x, k):
    return y, x, k


def send(value, chan_to=keep, day_to=lambda d: d):
    return lax.ppermute(value, AXES, pairs(chan_to, day_to))


def to_x(step):
    return lambda y, x, k: (y, (x + step) % 4, k)


def other_y(y, x, k):
    return 1 - y, x, k


def other_core(y, x, k):
    return y, x, 1 - k


def pack_kernel(cap, offs, weights, own, dm2, dm1, dp1, dp2, rest, lt_own, lt_hi, lt_lo, buf):
    buf[...] = jnp.zeros_like(buf)

    def place(day, skip, off):
        base, inside = off // 8 * 8, off % 8
        for r in range(0, 8, 2):

            @pl.when(inside == r)
            def _():
                def some(c, carry):
                    v = day[0, pl.ds(pl.multiple_of(skip + c * 32, 32), 32), :].astype(f32)
                    v = jnp.concatenate([v, jnp.zeros((8, 256), f32)], axis=0)
                    at = pl.ds(pl.multiple_of(base + c * 32, 8), 40)
                    buf[at, :] += pltpu.roll(v, r, 0) if r else v
                    return carry

                lax.fori_loop(0, (ROWS - skip) // 32, some, 0)

    place(own, OWN, offs[0])
    for i, day in enumerate((dm2, dm1, dp1, dp2)):
        place(day, 0, offs[i + 1])
    even = lax.broadcasted_iota(jnp.int32, (128, 256), 0) % 2 == 0

    def flip(v):
        return jnp.where(even, pltpu.roll(v, 127, 0), -pltpu.roll(v, 1, 0))

    first = own[0, :OWN, :].astype(f32)
    lt_own[0, :256, :] = first.T.astype(bf16)
    lt_own[0, 256:, :] = flip(first).T.astype(bf16)

    def chunk(c, carry):
        at = pl.multiple_of(c * 128, 128)
        v = buf[pl.ds(at, 128), :]
        rest[0, pl.ds(at, 128), :] = v.astype(bf16)
        row = lax.broadcasted_iota(jnp.int32, (128, 256), 0) + at
        w = jnp.full((128, 256), weights[0], f32)
        for i in range(1, 5):
            w = jnp.where(row >= offs[i], weights[i], w)
        for part, u in enumerate((v, flip(v))):
            t = (u * w).T
            hi = t.astype(bf16)
            lt_hi[0, pl.ds(part * 256, 256), pl.ds(at, 128)] = hi
            lt_lo[0, pl.ds(part * 256, 256), pl.ds(at, 128)] = (t - hi.astype(f32)).astype(bf16)
        return carry

    lax.fori_loop(0, cap // 128, chunk, 0)


def pack(cap, bins, offs, weights, days):
    first, n = bins
    smem = pl.BlockSpec(memory_space=pltpu.SMEM)
    return pl.pallas_call(
        functools.partial(pack_kernel, cap),
        grid=(n,),
        in_specs=[smem, smem] + [pl.BlockSpec((1, ROWS, 256), lambda b: (b, 0, 0))] * 5,
        out_specs=[
            pl.BlockSpec((1, cap, 256), lambda b: (b, 0, 0)),
            pl.BlockSpec((1, 512, OWN), lambda b: (b, 0, 0)),
            pl.BlockSpec((1, 512, cap), lambda b: (b, 0, 0)),
            pl.BlockSpec((1, 512, cap), lambda b: (b, 0, 0)),
        ],
        out_shape=[
            jax.ShapeDtypeStruct((n, cap, 256), bf16),
            jax.ShapeDtypeStruct((n, 512, OWN), bf16),
            jax.ShapeDtypeStruct((n, 512, cap), bf16),
            jax.ShapeDtypeStruct((n, 512, cap), bf16),
        ],
        scratch_shapes=[pltpu.VMEM((cap + ROWS + 8, 256), f32)],
        cost_estimate=pl.CostEstimate(flops=0, bytes_accessed=n * (5 * ROWS * 512 + cap * 2560), transcendentals=0),
    )(offs, weights, *days)


def tiles_kernel(bins, n, aliased, *refs):
    first, nb = bins
    cols, scale, lt_own, lt_hi, lt_lo = refs[:5]
    own = refs[5 : 5 + n]
    rest = refs[5 + n : 5 + 2 * n]
    out, own_buf, rest_buf, out_buf, in_sem, out_sem = refs[5 + 2 * n + aliased :]
    steps = nb * n

    def fetch(s, slot, run):
        b, t = s // n, s % n
        for i in range(n):

            @pl.when(t == i)
            def _():
                run(pltpu.make_async_copy(own[i].at[first + b], own_buf.at[slot], in_sem.at[slot, 0]))
                run(pltpu.make_async_copy(rest[i].at[b], rest_buf.at[slot], in_sem.at[slot, 1]))

    def put(s, slot):
        b, t = s // n, s % n
        col = pl.multiple_of(cols[t] * 256, 256)
        return pltpu.make_async_copy(
            out_buf.at[slot], out.at[first + b, :, :, pl.ds(col, 256)], out_sem.at[slot]
        )

    fetch(0, 0, lambda c: c.start())

    def step(s, carry):
        slot = s % 2

        @pl.when(s + 1 < steps)
        def _():
            fetch(s + 1, 1 - slot, lambda c: c.start())

        fetch(s, slot, lambda c: c.wait())

        @pl.when(s >= 2)
        def _():
            put(s - 2, slot).wait()

        b = s // n
        r = rest_buf[slot]
        for part in range(2):
            rows = pl.ds(part * 256, 256)
            acc = jnp.dot(lt_own[b, rows, :], own_buf[slot], preferred_element_type=f32) * scale[0]
            acc += jnp.dot(lt_hi[b, rows, :], r, preferred_element_type=f32)
            acc += jnp.dot(lt_lo[b, rows, :], r, preferred_element_type=f32)
            out_buf[slot, part] = acc.astype(bf16)
        put(s, slot).start()
        return carry

    lax.fori_loop(0, steps, step, 0)
    for s in range(max(steps - 2, 0), steps):
        put(s, s % 2).wait()


def tiles(cap, bins, cols, scale, left, own, rest, out):
    n, nb = len(own), bins[1]
    smem = pl.BlockSpec(memory_space=pltpu.SMEM)
    vmem = pl.BlockSpec(memory_space=pltpu.VMEM)
    anywhere = pl.BlockSpec(memory_space=pl.ANY)
    aliased = out is not None
    args = [cols, scale, *left, *own, *rest] + ([out] if aliased else [])
    return pl.pallas_call(
        functools.partial(tiles_kernel, bins, n, int(aliased)),
        in_specs=[smem, smem, vmem, vmem, vmem] + [anywhere] * (2 * n + int(aliased)),
        out_specs=anywhere,
        out_shape=jax.ShapeDtypeStruct((BINS, 2, 256, 9 * 256), bf16),
        scratch_shapes=[
            pltpu.VMEM((2, OWN, 256), bf16),
            pltpu.VMEM((2, cap, 256), bf16),
            pltpu.VMEM((2, 2, 256, 256), bf16),
            pltpu.SemaphoreType.DMA((2, 2)),
            pltpu.SemaphoreType.DMA((2,)),
        ],
        input_output_aliases={5 + 2 * n: 0} if aliased else {},
        cost_estimate=pl.CostEstimate(
            flops=nb * n * 2 * 512 * 256 * (2 * cap + OWN),
            bytes_accessed=nb * (n * (cap + OWN + 512) * 512 + 2048 * cap),
            transcendentals=0,
        ),
    )(*args)


def spread(block, x_index, core_index):
    swapped = send(block, other_y)
    down = send(jnp.where(x_index >= 1, block, swapped), to_x(-1))
    across = send(jnp.where(x_index >= 2, block, swapped), to_x(2))
    up = send(jnp.where(x_index >= 3, block, swapped), to_x(1))
    even = [block, down, across, up, swapped]
    odd = [jnp.where(core_index == 1, block, swapped), down, across, up]
    odd = [send(v, other_core) for v in odd]
    return even, odd


def path(cap, masked, offs, weights, scale, x_index, core_index):
    odd_cols = jnp.where(core_index == 0, jnp.array([1, 3, 5, 7]), jnp.array([7, 1, 3, 5])).astype(jnp.int32)
    own_even, own_odd = spread(masked[:, :OWN, :], x_index, core_index)
    out = None
    for bins in BIN_CHUNKS:
        first, nb = bins
        mine = masked[first : first + nb]
        days = [send(mine, day_to=lambda d, s=s: d + s) for s in (2, 1, -1, -2)]
        rest, *left = pack(cap, bins, offs, weights, [mine, *days])
        even, odd = spread(rest, x_index, core_index)
        near, far = jnp.array([0, 8], jnp.int32), jnp.array([2, 4, 6], jnp.int32)
        out = tiles(cap, bins, near, scale, left, [own_even[0], own_even[4]], [even[0], even[4]], out)
        out = tiles(cap, bins, odd_cols[:1], scale, left, own_odd[:1], odd[:1], out)
        out = tiles(cap, bins, far, scale, left, own_even[1:4], even[1:4], out)
        out = tiles(cap, bins, odd_cols[1:], scale, left, own_odd[1:], odd[1:], out)
    return out


def local(spectra, clean_counts, window_mask):
    chan = lax.axis_index("chan")
    day = lax.axis_index("day")
    x_index, core_index = (chan // 2) % 4, chan % 2
    days = clean_counts.shape[0]
    in_count = (jnp.arange(WIN, dtype=jnp.int32) < clean_counts[day]).astype(jnp.int32)
    keeper = (window_mask[0] * in_count[:, None]).astype(bf16)
    keep_rows = jnp.broadcast_to(keeper[:, None, :, None], (WIN, SEG * 2, 2, GROUP)).reshape(ROWS, 256)
    masked = spectra[0].reshape(BINS, ROWS, 256) * keep_rows[None]

    per_window = SEG * 2
    padded = jnp.pad(clean_counts, (2, 2))
    near = jnp.stack([padded[i : i + days] for i in range(SPAN)], axis=1)
    lens = per_window * near[:, jnp.array([2, 0, 1, 3, 4])]
    lens = lens.at[:, 0].set(jnp.maximum(lens[:, 0] - OWN, 0))
    need = jnp.max(jnp.sum(lens, axis=1))
    mine = lens[day]
    offs = jnp.concatenate([jnp.zeros((1,), jnp.int32), jnp.cumsum(mine)[:4]]).astype(jnp.int32)
    around = jnp.clip(day + jnp.array([0, -2, -1, 1, 2]), 0, days - 1)
    weights = f32(1.0) / (SEG * clean_counts[around].astype(f32))
    scale = weights[:1]
    which = sum((need > cap).astype(jnp.int32) for cap in CLASSES[:-1])
    branches = [
        lambda m, o, w, s, x, k, cap=cap: path(cap, m, o, w, s, x, k) for cap in CLASSES
    ]
    out = lax.switch(which, branches, masked, offs, weights, scale, x_index, core_index)
    return out[None]


def solution(mesh):
    in_specs = (P("day", None, None, None, None, "chan"), P(), P("day", None, "chan"))
    out_specs = P("day", None, None, "chan", None)
    return jax.shard_map(local, mesh=mesh, in_specs=in_specs, out_specs=out_specs, check_vma=False)
```

```python
import functools

import jax
import jax.numpy as jnp
from jax import lax
from jax.experimental import pallas as pl
from jax.experimental.pallas import tpu as pltpu
from jax.sharding import PartitionSpec as P


DAYS = 8
BINS = 4
WIN = 48
SEG = 3
STEP = SEG * 2
ROWS = WIN * STEP
OWN = 128
CLASSES = (640, 704)
FULL = 1344
NEIGHBOURS = (-2, -1, 1, 2)


AXES = ("chan", "day")
bf16 = jnp.bfloat16
f32 = jnp.float32
SMEM = pl.BlockSpec(memory_space=pltpu.SMEM)
VMEM = pl.BlockSpec(memory_space=pltpu.VMEM)
ANY = pl.BlockSpec(memory_space=pl.ANY)


def pairs(chan_to, day_to):
    route = []
    for c in range(16):
        for d in range(DAYS):
            c2 = chan_to(c // 8, (c // 2) % 4, c % 2)
            d2 = day_to(d)
            if 0 <= d2 < DAYS:
                route.append((c * DAYS + d, ((c2[0] * 4 + c2[1]) * 2 + c2[2]) * DAYS + d2))
    return route


def keep(y, x, k):
    return y, x, k


def send(value, chan_to=keep, day_to=lambda d: d):
    return lax.ppermute(value, AXES, pairs(chan_to, day_to))


def to_x(step):
    return lambda y, x, k: (y, (x + step) % 4, k)


def other_y(y, x, k):
    return 1 - y, x, k


def other_core(y, x, k):
    return y, x, 1 - k


def rows_near(counts, day):
    out = [jnp.maximum(STEP * counts[day] - OWN, 0)]
    for s in NEIGHBOURS:
        e = day + s
        inside = jnp.logical_and(e >= 0, e < DAYS)
        out.append(jnp.where(inside, STEP * counts[jnp.clip(e, 0, DAYS - 1)], 0))
    return out


def mask_kernel(counts, mask, spectra, masked, own, which):
    day = lax.axis_index("day")
    window = lax.broadcasted_iota(jnp.int32, (WIN, 256), 0)
    lane = lax.broadcasted_iota(jnp.int32, (WIN, 256), 1)
    valid = jnp.where(lane < 128, mask[:, 0:1], mask[:, 1:2])
    valid = jnp.where(window < counts[day], valid, 0).astype(bf16)
    row = lax.broadcasted_iota(jnp.int32, (ROWS, WIN), 0)
    first = lax.broadcasted_iota(jnp.int32, (ROWS, WIN), 1) * STEP
    of_window = jnp.where(jnp.logical_and(row >= first, row < first + STEP), 1, 0).astype(bf16)
    keep_rows = jnp.dot(of_window, valid, preferred_element_type=f32).astype(bf16)
    for b in range(BINS):
        v = spectra[b] * keep_rows
        masked[b] = v
        own[b] = v[:OWN]
    need = jnp.int32(0)
    for d in range(DAYS):
        need = jnp.maximum(need, sum(rows_near(counts, d)))
    which[0] = sum((need > cap).astype(jnp.int32) for cap in CLASSES)


def mask_own(counts, mask, spectra):
    return pl.pallas_call(
        mask_kernel,
        in_specs=[SMEM, VMEM, VMEM],
        out_specs=[VMEM, VMEM, SMEM],
        out_shape=[
            jax.ShapeDtypeStruct((BINS, ROWS, 256), bf16),
            jax.ShapeDtypeStruct((BINS, OWN, 256), bf16),
            jax.ShapeDtypeStruct((1,), jnp.int32),
        ],
    )(counts, mask, spectra)


def depth(cap):
    return 2 * (OWN + cap)


def pack_kernel(cap, counts, own, dm2, dm1, dp1, dp2, rest, left, buf):
    day = lax.axis_index("day")
    lens = rows_near(counts, day)
    offs = [jnp.int32(0)]
    for n in lens[:4]:
        offs.append(offs[-1] + n)
    around = [jnp.clip(day + s, 0, DAYS - 1) for s in (0, *NEIGHBOURS)]
    weights = [
        1.0 / (SEG * jnp.full((128, 256), counts[e], jnp.int32).astype(f32)) for e in around
    ]
    buf[...] = jnp.zeros_like(buf)

    def place(data, skip, off):
        base, inside = off // 8 * 8, off % 8
        for r in range(0, 8, 2):

            @pl.when(inside == r)
            def _():
                def some(c, carry):
                    v = data[0, pl.ds(pl.multiple_of(skip + c * 32, 32), 32), :].astype(f32)
                    v = jnp.concatenate([v, jnp.zeros((8, 256), f32)], axis=0)
                    at = pl.ds(pl.multiple_of(base + c * 32, 8), 40)
                    buf[at, :] += pltpu.roll(v, r, 0) if r else v
                    return carry

                lax.fori_loop(0, (ROWS - skip) // 32, some, 0)

    place(own, OWN, offs[0])
    for i, data in enumerate((dm2, dm1, dp1, dp2)):
        place(data, 0, offs[i + 1])
    iota = lax.broadcasted_iota(jnp.int32, (128, 256), 0)
    even = iota % 2 == 0
    full, half = cap // 128, cap % 128
    low = OWN + full * 128

    def halves(v, w):
        for part in range(2):
            u = v if part == 0 else jnp.where(even, pltpu.roll(v, 127, 0), -pltpu.roll(v, 1, 0))
            t = (u * w).T
            hi = t.astype(bf16)
            yield pl.ds(part * 256, 256), hi, (t - hi.astype(f32)).astype(bf16)

    def weight_at(row):
        w = weights[0]
        for i in range(1, 5):
            w = jnp.where(row >= offs[i], weights[i], w)
        return w

    for rows, hi, lo in halves(own[0, :OWN, :].astype(f32), weights[0]):
        left[0, rows, pl.ds(0, OWN)] = hi
        left[0, rows, pl.ds(low, OWN)] = lo

    def chunk(c, carry):
        at = pl.multiple_of(c * 128, 128)
        v = buf[pl.ds(at, 128), :]
        rest[0, pl.ds(at, 128), :] = v.astype(bf16)
        for rows, hi, lo in halves(v, weight_at(iota + at)):
            left[0, rows, pl.ds(pl.multiple_of(at + OWN, 128), 128)] = hi
            left[0, rows, pl.ds(pl.multiple_of(at + OWN + low, 128), 128)] = lo
        return carry

    lax.fori_loop(0, full, chunk, 0)
    if half:
        v = buf[pl.ds(full * 128, half), :]
        rest[0, pl.ds(full * 128, half), :] = v.astype(bf16)
        v = jnp.concatenate([v, v], axis=0)
        row = jnp.where(iota < half, iota, iota - half) + full * 128
        lane = lax.broadcasted_iota(jnp.int32, (256, 128), 1)
        for rows, hi, lo in halves(v, weight_at(row)):
            left[0, rows, pl.ds(2 * low, 128)] = jnp.where(lane < half, hi, lo)


def pack(cap, nb, counts, days):
    return pl.pallas_call(
        functools.partial(pack_kernel, cap),
        grid=(nb,),
        in_specs=[SMEM] + [pl.BlockSpec((1, ROWS, 256), lambda b: (b, 0, 0))] * 5,
        out_specs=[
            pl.BlockSpec((1, cap, 256), lambda b: (b, 0, 0)),
            pl.BlockSpec((1, 512, depth(cap)), lambda b: (b, 0, 0)),
        ],
        out_shape=[
            jax.ShapeDtypeStruct((nb, cap, 256), bf16),
            jax.ShapeDtypeStruct((nb, 512, depth(cap)), bf16),
        ],
        scratch_shapes=[pltpu.VMEM((cap + ROWS + 8, 256), f32)],
        cost_estimate=pl.CostEstimate(
            flops=nb * cap * 1024, bytes_accessed=nb * (5 * ROWS * 512 + cap * 2560), transcendentals=0
        ),
    )(counts, *days)


def tiles_kernel(cap, first, nb, columns, split, *refs):
    n = len(columns)
    left = refs[0]
    own = refs[1 : 1 + n]
    rest = refs[1 + n : 1 + 2 * n]
    out, right, out_buf, in_sem, out_sem = refs[-5:]
    core = lax.axis_index("chan") % 2
    steps = nb * n
    whole = cap // 128 * 128
    low = OWN + whole

    def fetch(s, slot, run):
        b, t = s // n, s % n
        for i in range(n):

            @pl.when(t == i)
            def _():
                mine, more = own[i].at[first + b], rest[i].at[b]
                moves = [(mine, 0, OWN), (mine, low, OWN)]
                moves += [(more.at[pl.ds(0, whole)], OWN, whole), (more.at[pl.ds(0, whole)], OWN + low, whole)]
                if cap > whole:
                    tail = more.at[pl.ds(whole, cap - whole)]
                    moves += [(tail, 2 * low + h * (cap - whole), cap - whole) for h in range(2)]
                for j, (src, at, size) in enumerate(moves):
                    run(pltpu.make_async_copy(src, right.at[slot, pl.ds(at, size)], in_sem.at[slot, j]))

    def put(s, slot):
        b, t = s // n, s % n
        col = jnp.int32(0)
        for i, (on_core_0, on_core_1) in enumerate(columns):
            col = jnp.where(t == i, jnp.where(core == 0, on_core_0, on_core_1), col)
        col = pl.multiple_of(col * 256, 256)
        return pltpu.make_async_copy(
            out_buf.at[slot], out.at[first + b, :, :, pl.ds(col, 256)], out_sem.at[slot]
        )

    fetch(0, 0, lambda c: c.start())

    def step(s, carry):
        slot = s % 2

        @pl.when(s + 1 < steps)
        def _():
            fetch(s + 1, 1 - slot, lambda c: c.start())

        fetch(s, slot, lambda c: c.wait())

        @pl.when(s >= 2)
        def _():
            put(s - 2, slot).wait()

        b = s // n

        def part_of(part, carry):
            rows = pl.ds(pl.multiple_of(part * 256, 256), 256)
            if split:

                def some(c, acc):
                    at = pl.multiple_of(c * 128, 128)
                    return acc + jnp.dot(left[b, rows, pl.ds(at, 128)], right[slot, pl.ds(at, 128), :], preferred_element_type=f32)

                acc = lax.fori_loop(0, depth(cap) // 128, some, jnp.zeros((256, 256), f32))
            else:
                acc = jnp.dot(left[b, rows, :], right[slot], preferred_element_type=f32)
            out_buf[slot, part] = acc.astype(bf16)
            return carry

        lax.fori_loop(0, 2, part_of, 0)
        put(s, slot).start()
        return carry

    lax.fori_loop(0, steps, step, 0)
    for s in range(steps - 2, steps):
        put(s, s % 2).wait()


def tiles(cap, bins, columns, left, own, rest, out, split=False):
    first, nb = bins
    n = len(columns)
    args = [left, *own, *rest] + ([] if out is None else [out])
    return pl.pallas_call(
        functools.partial(tiles_kernel, cap, first, nb, columns, split),
        in_specs=[VMEM] + [ANY] * (len(args) - 1),
        out_specs=ANY,
        out_shape=jax.ShapeDtypeStruct((BINS, 2, 256, 9 * 256), bf16),
        scratch_shapes=[
            pltpu.VMEM((2, depth(cap), 256), bf16),
            pltpu.VMEM((2, 2, 256, 256), bf16),
            pltpu.SemaphoreType.DMA((2, 6)),
            pltpu.SemaphoreType.DMA((2,)),
        ],
        input_output_aliases={} if out is None else {1 + 2 * n: 0},
        cost_estimate=pl.CostEstimate(
            flops=nb * n * 2 * 512 * 256 * depth(cap),
            bytes_accessed=nb * (n * (depth(cap) + 512) * 512 + 1024 * depth(cap)),
            transcendentals=0,
        ),
    )(*args)


def column_swap(block):
    return send(block, other_y)


def spread(block, swapped, x_index, core_index):
    first = jnp.where(core_index == 1, block, swapped)
    down = jnp.where(x_index >= 1, block, swapped)
    across = jnp.where(x_index >= 2, block, swapped)
    up = jnp.where(x_index >= 3, block, swapped)
    down = send(down, to_x(-1))
    up = send(up, to_x(1))
    across = send(across, to_x(2))
    odd = [send(v, other_core) for v in (first, down, across, up)]
    return [block, swapped, odd[0]], [down, across, up, *odd[1:]]


EARLY = ((0, 0), (8, 8), (1, 7))
LATE = ((2, 2), (4, 4), (6, 6), (3, 1), (5, 3), (7, 5))


def path(cap, chunks, masked, own, counts, x_index, core_index):
    slow = len(chunks) == 1
    own_early, own_late = spread(own, column_swap(own), x_index, core_index)
    out = None
    for bins in chunks:
        first, nb = bins
        mine = masked[first : first + nb]
        days = [send(mine, day_to=lambda d, s=s: d - s) for s in NEIGHBOURS]
        rest, left = pack(cap, nb, counts, [mine, *days])
        early, late = spread(rest, column_swap(rest), x_index, core_index)
        out = tiles(cap, bins, EARLY, left, own_early, early, out, slow)
        out = tiles(cap, bins, LATE, left, own_late, late, out, slow)
    return out


def local(spectra, clean_counts, window_mask):
    chan = lax.axis_index("chan")
    x_index, core_index = (chan // 2) % 4, chan % 2
    masked, own, which = mask_own(clean_counts, window_mask[0], spectra.reshape(BINS, ROWS, 256))

    def fast(cap):
        def run(*args):
            return path(cap, ((0, 2), (2, 2)), *args)

        return run

    branches = [fast(cap) for cap in CLASSES]
    branches.append(lambda *args: path(FULL, ((0, 4),), *args))
    out = lax.switch(which[0], branches, masked, own, clean_counts, x_index, core_index)
    return out[None]


def solution(mesh):
    in_specs = (P("day", None, None, None, None, "chan"), P(), P("day", None, "chan"))
    out_specs = P("day", None, None, "chan", None)
    return jax.shard_map(local, mesh=mesh, in_specs=in_specs, out_specs=out_specs, check_vma=False)
```
